32 devices in a mesh: slab: 8 (over z, y), sub: 4 (over x, core).
Axes of the slice: x: 2, y: 2, z: 4, core: 2. Of those that a mesh axis runs over, the one named last changes fastest.
Arguments:
- coefficients: bfloat16 [7, 6, 6, 64, 12, 128], P(None, None, None, 'slab', 'sub'), may hold values from -1 to 1
- earlier: float32 [30, 6, 64, 12, 128], P(None, None, 'slab', 'sub'), may hold values from -6 to 6
- start: float32 [6, 64, 12, 128], P(None, 'slab', 'sub'), may hold values from -8 to 8
- shifts: float32 [5], replicated, may hold values from -0.3 to 0.3
Outputs:
- new_basis: float32 [6, 6, 64, 12, 128], P(None, None, 'slab', 'sub')
- projection: float32 [30, 6], replicated
- triangle: float32 [6, 6], replicated
The draws below stay inside these ranges and needn't reach their ends.
All inputs are finite; a program needn't handle non-finite values.
Results may differ from the reference program's by a relative error of at most 0.0015.
Values may be sent and summed in bfloat16 or wider, within the bound.
A program may use at most 64 MiB of HBM per device.

```python
import jax
import jax.numpy as jnp
from jax import lax

COMP = 6
STENCIL = 7
DEPTH = 5
BLOCK = 6
EARLIER = 30
NZ = 64
NX = 12
NY = 128


def earlier_basis(key):
    base_key = jax.random.fold_in(key, 7)
    dims = (EARLIER, COMP, NZ, NX, NY)
    values = jnp.clip(jax.random.normal(base_key, dims, jnp.float32), -6.0, 6.0)
    return values


def draw_earlier(key, part):
    return earlier_basis(key)


def draw_start(key, part):
    basis_values = earlier_basis(key)
    mixing = jnp.clip(jax.random.normal(jax.random.fold_in(key, 11), (EARLIER,), jnp.float32), -3.0, 3.0)
    jitter = jnp.clip(jax.random.normal(jax.random.fold_in(key, 13), (COMP, NZ, NX, NY), jnp.float32), -6.0, 6.0)
    combined = 0.3 * jnp.tensordot(mixing, basis_values, axes=1) + 0.5 * jitter
    return jnp.clip(combined, -8.0, 8.0)


def block_scale(stream_key, shape, pieces, least, largest):
    def one(axis_at, parts):
        draws = jax.random.uniform(jax.random.fold_in(jax.random.fold_in(stream_key, 6), axis_at), (parts,), jnp.float32, least / len(pieces), largest / len(pieces))
        return jnp.repeat(jnp.exp(draws), shape[axis_at] // parts).reshape((-1,) + (1,) * (len(shape) - axis_at - 1))

    loudness = one(*pieces[0])
    for cut in pieces[1:]:
        loudness = loudness * one(*cut)
    return loudness


def normal_values(stream_key, shape, scale, most, cuts=(), held_as=jnp.bfloat16):
    factor_of = block_scale(stream_key, shape, cuts, -0.22, 0.18) if cuts else 1.0
    values = jax.random.normal(stream_key, shape, jnp.float32) * scale * factor_of
    return jnp.minimum(jnp.maximum(values, -most), most).astype(held_as)


def setup_inputs(seed: int = 0) -> dict:
    key_of = jax.random.split(jax.random.key(seed), 5)
    return {
        "coefficients": normal_values(key_of[0], (STENCIL, COMP, COMP, NZ, NX, NY), (STENCIL * COMP) ** -0.5, 1.0, ((3, 8), (4, 4))),
        "earlier": draw_earlier(jax.random.fold_in(key_of[4], 71), 0),
        "start": draw_start(jax.random.fold_in(key_of[4], 71), 0),
        "shifts": jnp.clip(jax.random.uniform(key_of[3], (DEPTH,), jnp.float32, -0.3, 0.3), -0.3, 0.3),
    }


def nearby_fields(padded):
    center = padded[:, 1:-1, 1:-1]
    zeros_edge = jnp.zeros_like(center[..., :1])
    lower_y = jnp.concatenate([zeros_edge, center[..., :-1]], axis=3)
    upper_y = jnp.concatenate([center[..., 1:], zeros_edge], axis=3)
    return [center, padded[:, :-2, 1:-1], padded[:, 2:, 1:-1], padded[:, 1:-1, :-2], padded[:, 1:-1, 2:], lower_y, upper_y]

def apply_padded(coefficients, padded, theta):
    fields = nearby_fields(padded)
    result = (1.0 - theta) * fields[0]
    for coupling in range(len(fields)):
        result = result + jnp.sum(coefficients[coupling] * fields[coupling][None], axis=1)
    return result

def reference(coefficients, earlier, start, shifts):
    current = start
    vectors = [start]
    for step in range(DEPTH):
        padded = jnp.pad(current, ((0, 0), (1, 1), (1, 1), (0, 0)))
        current = apply_padded(coefficients, padded, shifts[step])
        vectors.append(current)
    basis = jnp.stack(vectors)
    flat = basis.reshape(BLOCK, -1)
    earlier_flat = earlier.reshape(EARLIER, -1)
    count = flat.shape[1]
    projection = jnp.dot(earlier_flat, flat.T, precision=lax.Precision.HIGHEST) / count
    rest = flat - jnp.dot(projection.T, earlier_flat, precision=lax.Precision.HIGHEST)
    gram = jnp.dot(rest, rest.T, precision=lax.Precision.HIGHEST) / count
    lower = jnp.linalg.cholesky(gram)
    new_flat = lax.linalg.triangular_solve(lower, rest, left_side=True, lower=True)
    return (new_flat.reshape(basis.shape), projection, lower.T)
```

```python
import functools

import jax
import jax.numpy as jnp
from jax import lax
from jax.experimental import pallas as pl
from jax.experimental.pallas import tpu as pltpu
from jax.sharding import PartitionSpec as P

MESH = pl.DeviceIdType.MESH
LANES = 128
ROWS = 8


def dot(a, b, nt=False):
    return lax.dot_general(
        a, b, (((1,), (1 if nt else 0,)), ((), ())),
        precision=lax.Precision.HIGHEST, preferred_element_type=jnp.float32,
    )


def iota(shape, dim):
    return lax.broadcasted_iota(jnp.int32, shape, dim)


def onehot(shape, test):
    return jnp.where(test(iota(shape, 0), iota(shape, 1)), 1.0, 0.0).astype(jnp.float32)


def factors(count):
    found = []
    while count > 1:
        size = max(f for f in range(2, min(count, 8) + 1) if count % f == 0) if any(
            count % f == 0 for f in range(2, min(count, 8) + 1)
        ) else count
        found.append(size)
        count //= size
    return found


def stages_of(sizes):
    found = []
    for axis, count in sizes:
        stride = 1
        for size in factors(count):
            found.append((axis, stride, size))
            stride *= size
    return found


def side_by_side(value):
    count, width = value.shape[0], value.shape[1]
    return jnp.concatenate(
        [value[:, x].reshape(count * ROWS, LANES) for x in range(width)], axis=1
    )


def kernel(
    sizes, coef_hbm, early_hbm, start_hbm, shifts_ref, new_ref, proj_ref, tri_ref,
    coef_in, coef, edge_coef, allv, acc_ref, halo_x, halo_z, send_z, ee, mine, gathered,
    in_sem, halo_send, halo_recv, red_send, red_recv,
):
    depth = shifts_ref.shape[0]
    earlier, comp, width = early_hbm.shape[:3]
    block = depth + 1
    count = comp * width * ROWS * LANES * sizes[0][1] * sizes[1][1]
    stages = stages_of(sizes)
    place = {axis: lax.axis_index(axis) for axis, _ in sizes}
    slab, sub = sizes[0], sizes[1]

    def peer(stage, offset):
        axis, stride, size = stage
        digit = lax.rem(place[axis] // stride, size)
        other = lax.rem(digit + offset, size)
        return axis, digit, other, place[axis] + (other - digit) * stride

    copy_start = pltpu.make_async_copy(start_hbm, allv.at[earlier], in_sem.at[0])
    copy_coef = pltpu.make_async_copy(coef_hbm, coef_in, in_sem.at[1])
    copy_early = pltpu.make_async_copy(early_hbm, allv.at[pl.ds(0, earlier)], in_sem.at[2])
    copy_start.start()
    copy_coef.start()
    copy_early.start()

    halo_x[...] = jnp.zeros_like(halo_x)
    halo_z[...] = jnp.zeros_like(halo_z)
    send_z[...] = jnp.zeros_like(send_z)
    ee[...] = jnp.zeros_like(ee)

    barrier = pltpu.get_barrier_semaphore()
    expected = 0
    for stage in stages:
        for offset in range(1, stage[2]):
            axis, _, _, target = peer(stage, offset)
            pl.semaphore_signal(barrier, inc=1, device_id={axis: target}, device_id_type=MESH)
            expected += 1
    extra = [(axis, n) for axis, n in sizes if len(factors(n)) > 1]
    for axis, n in extra:
        for off in (-1, 1):
            there = jnp.logical_and(place[axis] + off >= 0, place[axis] + off < n)

            @pl.when(there)
            def _():
                pl.semaphore_signal(
                    barrier, inc=1, device_id={axis: place[axis] + off}, device_id_type=MESH
                )

    def halo_copy(step, kind, side):
        axis, n = (slab, sub)[kind]
        if kind == 0:
            src, dst = send_z.at[step, side], halo_z.at[step, side]
        else:
            src = allv.at[earlier + step, :, width - 1 if side == 0 else 0]
            dst = halo_x.at[step, side]
        target = place[axis] + (1 if side == 0 else -1)
        return pltpu.make_async_remote_copy(
            src_ref=src, dst_ref=dst,
            send_sem=halo_send.at[step, kind, side], recv_sem=halo_recv.at[step, kind, side],
            device_id={axis: target}, device_id_type=MESH,
        )

    def has(kind, side, sending):
        axis, n = (slab, sub)[kind]
        upward = (side == 0) == sending
        return place[axis] < n - 1 if upward else place[axis] > 0

    def pack(step):
        for e in range(comp):
            for x in range(width):
                row = 4 * e + x
                tile = allv.at[earlier + step, e, x]
                send_z[step, 0, row:row + 1, :] = tile[ROWS - 1:ROWS, :]
                send_z[step, 1, row:row + 1, :] = tile[0:1, :]

    def send(step):
        for kind in (0, 1):
            for side in (0, 1):
                @pl.when(has(kind, side, True))
                def _():
                    halo_copy(step, kind, side).start()

    copy_start.wait()
    pack(0)
    for axis, n in extra:
        for off in (-1, 1):
            there = jnp.logical_and(place[axis] + off >= 0, place[axis] + off < n)

            @pl.when(there)
            def _():
                pl.semaphore_wait(barrier, 1)
    pl.semaphore_wait(barrier, expected)
    send(0)

    copy_coef.wait()

    @pl.loop(0, comp)
    def _(c):
        for d in range(coef.shape[0]):
            coef[d, c] = coef_in[d, c].astype(jnp.float32)
        edge_coef[c] = jnp.zeros_like(edge_coef[c])
        for e in range(comp):
            for x in range(width):
                edge_coef[c, e, x:x + 1, :] = coef[1, c, e, x, 0:1, :]
                edge_coef[c, e, 4 + x:5 + x, :] = coef[2, c, e, x, ROWS - 1:ROWS, :]

    copy_early.wait()

    def self_products(c):
        part = side_by_side(allv[pl.ds(0, earlier), c])
        ee[...] += dot(part, part, nt=True)

    row3 = iota((width, ROWS, LANES), 1)
    lane3 = iota((width, ROWS, LANES), 2)
    row2 = iota((ROWS, LANES), 0)
    zero_tile = jnp.zeros((1, ROWS, LANES), jnp.float32)

    @pl.loop(0, depth)
    def _(step):
        acc = (1.0 - shifts_ref[step]) * allv[earlier + step]
        for e in range(comp):
            v = allv[earlier + step, e]
            near = [
                v,
                jnp.where(row3 > 0, pltpu.roll(v, 1, 1), 0.0),
                jnp.where(row3 < ROWS - 1, pltpu.roll(v, ROWS - 1, 1), 0.0),
                jnp.concatenate([zero_tile, v[:-1]], axis=0),
                jnp.concatenate([v[1:], zero_tile], axis=0),
                jnp.where(lane3 > 0, pltpu.roll(v, 1, 2), 0.0),
                jnp.where(lane3 < LANES - 1, pltpu.roll(v, LANES - 1, 2), 0.0),
            ]
            for d in range(len(near)):
                acc = acc + coef[d, :, e] * near[d][None]
        acc_ref[...] = acc

        @pl.loop(step * comp // depth, (step + 1) * comp // depth)
        def _(c):
            self_products(c)

        for kind in (0, 1):
            for side in (0, 1):
                @pl.when(has(kind, side, False))
                def _():
                    halo_copy(step, kind, side).wait_recv()

        edge = jnp.zeros((comp, ROWS, LANES), jnp.float32)
        low = jnp.zeros((comp, ROWS, LANES), jnp.float32)
        high = jnp.zeros((comp, ROWS, LANES), jnp.float32)
        for e in range(comp):
            base = ROWS * (e // 2)
            below = halo_z[step, 0, base:base + ROWS, :]
            above = halo_z[step, 1, base:base + ROWS, :]
            if e % 2 == 0:
                above = pltpu.roll(above, 4, 0)
            else:
                below = pltpu.roll(below, 4, 0)
            edge = edge + edge_coef[:, e] * jnp.where(row2 < 4, below, above)[None]
            low = low + coef[3, :, e, 0] * halo_x[step, 0, e][None]
            high = high + coef[4, :, e, width - 1] * halo_x[step, 1, e][None]
        for c in range(comp):
            for x in range(width):
                value = acc_ref[c, x]
                if x == 0:
                    value = value + low[c]
                if x == width - 1:
                    value = value + high[c]
                value = value + jnp.where(
                    row2 == 0, edge[c, x:x + 1, :],
                    jnp.where(row2 == ROWS - 1, edge[c, 4 + x:5 + x, :], 0.0),
                )
                allv[earlier + step + 1, c, x] = value

        @pl.when(step < depth - 1)
        def _():
            pack(step + 1)
            send(step + 1)

    total = earlier + block
    cross = jnp.zeros((block * ROWS, total * ROWS), jnp.float32)
    for c in range(comp):
        part = side_by_side(allv[:, c])
        cross = cross + dot(part[earlier * ROWS:], part, nt=True)

    def diagonal(value):
        r, q = iota(value.shape, 0), iota(value.shape, 1)
        return jnp.where((r & 7) == (q & 7), value, 0.0)

    wide = dot(diagonal(cross), onehot((total * ROWS, LANES), lambda r, q: (r >> 3) == q))
    mine[0] = dot(onehot((ROWS, block * ROWS), lambda r, q: (q >> 3) == r), wide)
    span = earlier * ROWS
    wide = dot(diagonal(ee[...]), onehot((span, LANES), lambda r, q: (r >> 3) == (q & 31)))
    wide = jnp.where((iota(wide.shape, 0) >> 6) == (iota(wide.shape, 1) >> 5), wide, 0.0)
    mine[1] = dot(onehot((ROWS, span), lambda r, q: ((q >> 3) & 7) == r), wide)

    for at, stage in enumerate(stages):
        size = stage[2]
        source = mine.at[pl.ds(2 * at, 2)]

        def move(offset, sending):
            axis, digit, other, target = peer(stage, offset)
            return pltpu.make_async_remote_copy(
                src_ref=source, dst_ref=gathered.at[at, digit],
                send_sem=red_send.at[at, other],
                recv_sem=red_recv.at[at, digit if sending else other],
                device_id={axis: target}, device_id_type=MESH,
            )

        for offset in range(1, size):
            move(offset, True).start()
        digit = peer(stage, 0)[1]
        gathered[at, digit] = source[...]
        for offset in range(1, size):
            move(offset, False).wait_recv()
        whole = gathered[at, 0]
        for other in range(1, size):
            whole = whole + gathered[at, other]
        mine[2 * at + 2:2 * at + 4] = whole
    sums = mine[2 * len(stages):2 * len(stages) + 2] * (1.0 / count)

    lane = iota((ROWS, LANES), 1)
    proj_t = jnp.where(lane < earlier, sums[0], 0.0)
    gram = pltpu.roll(sums[0], LANES - earlier, 1)[:, :ROWS]
    packed = sums[1]
    square = jnp.concatenate(
        [packed] + [pltpu.roll(packed, LANES - 32 * g, 1) for g in range(1, 4)], axis=0
    )
    sr, sl = iota(square.shape, 0), iota(square.shape, 1)
    square = jnp.where(sl < 32, square, 0.0) - jnp.where(sr == sl, 2.0, 0.0)
    gram = gram + dot(dot(proj_t[:, :32], square), proj_t, nt=True)

    upper = gram
    inverse = onehot((ROWS, ROWS), lambda r, q: r == q)
    r8 = iota((ROWS, ROWS), 0)
    q8 = iota((ROWS, ROWS), 1)
    for p in range(block):
        pivot = upper[p:p + 1, p:p + 1]
        scale = lax.rsqrt(pivot)
        scale = scale * (1.5 - 0.5 * pivot * scale * scale)
        column = upper[:, p:p + 1] * scale
        row_u, row_i = upper[p:p + 1, :] * scale, inverse[p:p + 1, :] * scale
        upper = jnp.where(r8 == p, row_u, jnp.where(r8 > p, upper - column * row_u, upper))
        inverse = jnp.where(r8 == p, row_i, jnp.where(r8 > p, inverse - column * row_i, inverse))
    tri_ref[...] = jnp.where(q8 >= r8, upper, 0.0)[:block, :block]
    proj_ref[...] = proj_t[:block, :earlier]

    pick = onehot((ROWS, LANES), lambda r, q: q == r + earlier)
    mix = dot(inverse, pick - proj_t)
    mix = dot(onehot((block * ROWS, ROWS), lambda r, q: (r >> 3) == q), mix)
    mix = diagonal(dot(mix, onehot((LANES, total * ROWS), lambda r, q: (q >> 3) == r)))
    for c in range(comp):
        out = dot(mix, side_by_side(allv[:, c]))
        for x in range(width):
            new_ref[:, c, x] = out[:, LANES * x:LANES * (x + 1)].reshape(block, ROWS, LANES)

    @pl.loop(0, depth)
    def _(step):
        for kind in (0, 1):
            for side in (0, 1):
                @pl.when(has(kind, side, True))
                def _():
                    halo_copy(step, kind, side).wait_send()

    for at, stage in enumerate(stages):
        for offset in range(1, stage[2]):
            axis, digit, other, target = peer(stage, offset)
            pltpu.make_async_remote_copy(
                src_ref=mine.at[pl.ds(2 * at, 2)], dst_ref=gathered.at[at, digit],
                send_sem=red_send.at[at, other], recv_sem=red_recv.at[at, digit],
                device_id={axis: target}, device_id_type=MESH,
            ).wait_send()


def body(sizes, coefficients, earlier, start, shifts):
    coefficients = jnp.transpose(coefficients, (0, 1, 2, 4, 3, 5))
    earlier = jnp.transpose(earlier, (0, 1, 3, 2, 4))
    start = jnp.transpose(start, (0, 2, 1, 3))
    depth, count = shifts.shape[0], earlier.shape[0]
    block = depth + 1
    kinds, comp, _, width, rows, lanes = coefficients.shape
    stages = stages_of(sizes)
    most = max(stage[2] for stage in stages)
    f32 = jnp.float32
    anywhere = pl.BlockSpec(memory_space=pl.ANY)
    vmem = pl.BlockSpec(memory_space=pltpu.VMEM)
    new, proj, tri = pl.pallas_call(
        functools.partial(kernel, sizes),
        out_shape=(
            jax.ShapeDtypeStruct((block, comp, width, rows, lanes), f32),
            jax.ShapeDtypeStruct((block, count), f32),
            jax.ShapeDtypeStruct((block, block), f32),
        ),
        in_specs=[anywhere, anywhere, anywhere, pl.BlockSpec(memory_space=pltpu.SMEM)],
        out_specs=(vmem, vmem, vmem),
        scratch_shapes=[
            pltpu.VMEM(coefficients.shape, coefficients.dtype),
            pltpu.VMEM(coefficients.shape, f32),
            pltpu.VMEM((comp, comp, rows, lanes), f32),
            pltpu.VMEM((count + block, comp, width, rows, lanes), f32),
            pltpu.VMEM((comp, width, rows, lanes), f32),
            pltpu.VMEM((depth, 2, comp, rows, lanes), f32),
            pltpu.VMEM((depth, 2, 4 * comp, lanes), f32),
            pltpu.VMEM((depth, 2, 4 * comp, lanes), f32),
            pltpu.VMEM((count * rows, count * rows), f32),
            pltpu.VMEM((2 * len(stages) + 2, rows, lanes), f32),
            pltpu.VMEM((len(stages), most, 2, rows, lanes), f32),
            pltpu.SemaphoreType.DMA((3,)),
            pltpu.SemaphoreType.DMA((depth, 2, 2)),
            pltpu.SemaphoreType.DMA((depth, 2, 2)),
            pltpu.SemaphoreType.DMA((len(stages), most)),
            pltpu.SemaphoreType.DMA((len(stages), most)),
        ],
        compiler_params=pltpu.CompilerParams(collective_id=0, has_side_effects=True),
        name="powers",
    )(coefficients, earlier, start, shifts)
    return jnp.transpose(new, (0, 1, 3, 2, 4)), proj.T, tri


def solution(mesh):
    sizes = (("slab", mesh.shape["slab"]), ("sub", mesh.shape["sub"]))
    placed = (
        P(None, None, None, "slab", "sub", None),
        P(None, None, "slab", "sub", None),
        P(None, "slab", "sub", None),
        P(),
    )
    return jax.shard_map(
        functools.partial(body, sizes),
        mesh=mesh,
        in_specs=placed,
        out_specs=(P(None, None, "slab", "sub", None), P(), P()),
        check_vma=False,
    )
```

```python
import functools

import jax
import jax.numpy as jnp
from jax import lax
from jax.experimental import pallas as pl
from jax.experimental.pallas import tpu as pltpu
from jax.sharding import PartitionSpec as P

MESH = pl.DeviceIdType.MESH
LANES = 128
ROWS = 8


def dot(a, b, nt=False):
    return lax.dot_general(
        a, b, (((1,), (1 if nt else 0,)), ((), ())),
        precision=lax.Precision.HIGHEST, preferred_element_type=jnp.float32,
    )


def iota(shape, dim):
    return lax.broadcasted_iota(jnp.int32, shape, dim)


def onehot(shape, test):
    return jnp.where(test(iota(shape, 0), iota(shape, 1)), 1.0, 0.0).astype(jnp.float32)


def factors(count):
    found = []
    while count > 1:
        size = max(f for f in range(2, min(count, 8) + 1) if count % f == 0) if any(
            count % f == 0 for f in range(2, min(count, 8) + 1)
        ) else count
        found.append(size)
        count //= size
    return found


def stages_of(sizes):
    found = []
    for axis, count in sizes:
        stride = 1
        for size in factors(count):
            found.append((axis, stride, size))
            stride *= size
    return found


def diagonal(value):
    r, q = iota(value.shape, 0), iota(value.shape, 1)
    return jnp.where((r & 7) == (q & 7), value, 0.0)


def split(value):
    first = value.astype(jnp.bfloat16)
    left = value - first.astype(jnp.float32)
    second = left.astype(jnp.bfloat16)
    third = (left - second.astype(jnp.float32)).astype(jnp.bfloat16)
    return [first, second, third]


def dot_pieces(a, b, nt=False):
    found = None
    rows = a[0].shape[0]
    for at in (2, 1, 0):
        left = jnp.concatenate(a[: 3 - at], axis=0)
        part = lax.dot_general(
            left, b[at], (((1,), (1 if nt else 0,)), ((), ())),
            preferred_element_type=jnp.float32,
        )
        for i in reversed(range(3 - at)):
            piece = part[i * rows:(i + 1) * rows]
            found = piece if found is None else found + piece
    return found


def side_by_side(value):
    count, width = value.shape[0], value.shape[1]
    return jnp.concatenate(
        [value[:, x].reshape(count * ROWS, LANES) for x in range(width)], axis=1
    )


def kernel(
    sizes, coef_hbm, early_hbm, start_hbm, shifts_ref, new_ref, small_ref,
    coef_in, coef, edge_coef, allv, pieces, acc_ref, halo_x, halo_z, send_z, ee, sums_ref,
    mine, gathered,
    in_sem, halo_send, halo_recv, red_send, red_recv,
):
    depth = shifts_ref.shape[0]
    earlier, comp, width = early_hbm.shape[:3]
    block = depth + 1
    count = comp * width * ROWS * LANES * sizes[0][1] * sizes[1][1]
    stages = stages_of(sizes)
    place = {axis: lax.axis_index(axis) for axis, _ in sizes}
    slab, sub = sizes[0], sizes[1]

    def peer(stage, offset):
        axis, stride, size = stage
        digit = lax.rem(place[axis] // stride, size)
        other = lax.rem(digit + offset, size)
        return axis, digit, other, place[axis] + (other - digit) * stride

    copy_start = pltpu.make_async_copy(start_hbm, allv.at[earlier], in_sem.at[0])
    copy_coef = pltpu.make_async_copy(coef_hbm, coef_in, in_sem.at[1])
    copy_early = pltpu.make_async_copy(early_hbm, allv.at[pl.ds(0, earlier)], in_sem.at[2])
    copy_start.start()
    copy_coef.start()
    copy_early.start()

    halo_x[...] = jnp.zeros_like(halo_x)
    halo_z[...] = jnp.zeros_like(halo_z)
    send_z[...] = jnp.zeros_like(send_z)
    ee[...] = jnp.zeros_like(ee)
    mine[0] = jnp.zeros_like(mine[0])
    sums_ref[...] = jnp.zeros_like(sums_ref)
    for k in range(1, block):
        allv[earlier + k] = jnp.zeros_like(allv[earlier + k])

    barrier = pltpu.get_barrier_semaphore()
    expected = 0
    for stage in stages:
        for offset in range(1, stage[2]):
            axis, _, _, target = peer(stage, offset)
            pl.semaphore_signal(barrier, inc=1, device_id={axis: target}, device_id_type=MESH)
            expected += 1
    extra = [(axis, n) for axis, n in sizes if len(factors(n)) > 1]
    for axis, n in extra:
        for off in (-1, 1):
            there = jnp.logical_and(place[axis] + off >= 0, place[axis] + off < n)

            @pl.when(there)
            def _():
                pl.semaphore_signal(
                    barrier, inc=1, device_id={axis: place[axis] + off}, device_id_type=MESH
                )

    def halo_copy(step, kind, side):
        axis, n = (slab, sub)[kind]
        if kind == 0:
            src, dst = send_z.at[step, side], halo_z.at[step, side]
        else:
            src = allv.at[earlier + step, :, width - 1 if side == 0 else 0]
            dst = halo_x.at[step, side]
        target = place[axis] + (1 if side == 0 else -1)
        return pltpu.make_async_remote_copy(
            src_ref=src, dst_ref=dst,
            send_sem=halo_send.at[step, kind, side], recv_sem=halo_recv.at[step, kind, side],
            device_id={axis: target}, device_id_type=MESH,
        )

    def has(kind, side, sending):
        axis, n = (slab, sub)[kind]
        upward = (side == 0) == sending
        return place[axis] < n - 1 if upward else place[axis] > 0

    def pack(step):
        for e in range(comp):
            for x in range(width):
                row = 4 * e + x
                tile = allv.at[earlier + step, e, x]
                send_z[step, 0, row:row + 1, :] = tile[ROWS - 1:ROWS, :]
                send_z[step, 1, row:row + 1, :] = tile[0:1, :]

    def send(step):
        for kind in (0, 1):
            for side in (0, 1):
                @pl.when(has(kind, side, True))
                def _():
                    halo_copy(step, kind, side).start()

    copy_start.wait()
    pack(0)
    for axis, n in extra:
        for off in (-1, 1):
            there = jnp.logical_and(place[axis] + off >= 0, place[axis] + off < n)

            @pl.when(there)
            def _():
                pl.semaphore_wait(barrier, 1)
    pl.semaphore_wait(barrier, expected)
    send(0)

    copy_coef.wait()

    @pl.loop(0, comp)
    def _(c):
        for d in range(coef.shape[0]):
            coef[d, c] = coef_in[d, c].astype(jnp.float32)
        edge_coef[c] = jnp.zeros_like(edge_coef[c])
        for e in range(comp):
            for x in range(width):
                edge_coef[c, e, x:x + 1, :] = coef[1, c, e, x, 0:1, :]
                edge_coef[c, e, 4 + x:5 + x, :] = coef[2, c, e, x, ROWS - 1:ROWS, :]

    copy_early.wait()

    def self_products(c):
        parts = split(side_by_side(allv[pl.ds(0, earlier), c]))
        for at, part in enumerate(parts):
            pieces[at, c] = part
        ee[...] += dot_pieces(parts, [parts[0], parts[1], parts[2]], nt=True)

    def cross_products(k):
        total, group = earlier + block, 6
        w = allv[earlier + k]
        for low in range(0, total, group):
            high = min(low + group, total)
            part = jnp.sum(w[None] * allv[low:high], axis=(1, 2))
            sums_ref[low:high, :] = jnp.sum(part, axis=1)
        line = dot(jnp.ones((ROWS, LANES), jnp.float32), sums_ref[...], nt=True)
        mine[0, pl.ds(k, 1), :] = line[0:1]

    def self_finish():
        span = earlier * ROWS
        wide = dot(diagonal(ee[...]), onehot((span, LANES), lambda r, q: (r >> 3) == (q & 31)))
        wide = jnp.where((iota(wide.shape, 0) >> 6) == (iota(wide.shape, 1) >> 5), wide, 0.0)
        mine[1] = dot(onehot((ROWS, span), lambda r, q: ((q >> 3) & 7) == r), wide)

    row3 = iota((width, ROWS, LANES), 1)
    lane3 = iota((width, ROWS, LANES), 2)
    row2 = iota((ROWS, LANES), 0)
    zero_tile = jnp.zeros((1, ROWS, LANES), jnp.float32)

    @pl.loop(0, depth)
    def _(step):
        acc = (1.0 - shifts_ref[step]) * allv[earlier + step]
        for e in range(comp):
            v = allv[earlier + step, e]
            near = [
                v,
                jnp.where(row3 > 0, pltpu.roll(v, 1, 1), 0.0),
                jnp.where(row3 < ROWS - 1, pltpu.roll(v, ROWS - 1, 1), 0.0),
                jnp.concatenate([zero_tile, v[:-1]], axis=0),
                jnp.concatenate([v[1:], zero_tile], axis=0),
                jnp.where(lane3 > 0, pltpu.roll(v, 1, 2), 0.0),
                jnp.where(lane3 < LANES - 1, pltpu.roll(v, LANES - 1, 2), 0.0),
            ]
            for d in range(len(near)):
                acc = acc + coef[d, :, e] * near[d][None]
        acc_ref[...] = acc

        cross_products(step)

        @pl.loop(
            step * comp // (depth - 1), jnp.minimum((step + 1) * comp // (depth - 1), comp)
        )
        def _(c):
            self_products(c)

        @pl.when(step == depth - 1)
        def _():
            self_finish()

        for kind in (0, 1):
            for side in (0, 1):
                @pl.when(has(kind, side, False))
                def _():
                    halo_copy(step, kind, side).wait_recv()

        edge = jnp.zeros((comp, ROWS, LANES), jnp.float32)
        low = jnp.zeros((comp, ROWS, LANES), jnp.float32)
        high = jnp.zeros((comp, ROWS, LANES), jnp.float32)
        for e in range(comp):
            base = ROWS * (e // 2)
            below = halo_z[step, 0, base:base + ROWS, :]
            above = halo_z[step, 1, base:base + ROWS, :]
            if e % 2 == 0:
                above = pltpu.roll(above, 4, 0)
            else:
                below = pltpu.roll(below, 4, 0)
            edge = edge + edge_coef[:, e] * jnp.where(row2 < 4, below, above)[None]
            low = low + coef[3, :, e, 0] * halo_x[step, 0, e][None]
            high = high + coef[4, :, e, width - 1] * halo_x[step, 1, e][None]
        for c in range(comp):
            for x in range(width):
                value = acc_ref[c, x]
                if x == 0:
                    value = value + low[c]
                if x == width - 1:
                    value = value + high[c]
                value = value + jnp.where(
                    row2 == 0, edge[c, x:x + 1, :],
                    jnp.where(row2 == ROWS - 1, edge[c, 4 + x:5 + x, :], 0.0),
                )
                allv[earlier + step + 1, c, x] = value

        @pl.when(step < depth - 1)
        def _():
            pack(step + 1)
            send(step + 1)

    cross_products(depth)
    total = earlier + block

    for at, stage in enumerate(stages):
        size = stage[2]
        source = mine.at[pl.ds(2 * at, 2)]

        def move(offset, sending):
            axis, digit, other, target = peer(stage, offset)
            return pltpu.make_async_remote_copy(
                src_ref=source, dst_ref=gathered.at[at, digit],
                send_sem=red_send.at[at, other],
                recv_sem=red_recv.at[at, digit if sending else other],
                device_id={axis: target}, device_id_type=MESH,
            )

        for offset in range(1, size):
            move(offset, True).start()
        digit = peer(stage, 0)[1]
        gathered[at, digit] = source[...]
        for offset in range(1, size):
            move(offset, False).wait_recv()
        whole = gathered[at, 0]
        for other in range(1, size):
            whole = whole + gathered[at, other]
        mine[2 * at + 2:2 * at + 4] = whole
    sums = mine[2 * len(stages):2 * len(stages) + 2] * (1.0 / count)

    row, lane = iota((ROWS, LANES), 0), iota((ROWS, LANES), 1)
    proj_t = jnp.where(lane < earlier, sums[0], 0.0)
    known = jnp.where(lane < earlier + row, sums[0], 0.0)
    pick = onehot((ROWS, LANES), lambda r, q: q == r + earlier)
    gram = jnp.where(lane <= earlier + row, sums[0], 0.0)
    gram = pltpu.roll(gram, LANES - earlier, 1)[:, :ROWS]
    packed = sums[1]
    square = jnp.concatenate(
        [packed] + [pltpu.roll(packed, LANES - 32 * g, 1) for g in range(1, 4)], axis=0
    )
    sr, sl = iota(square.shape, 0), iota(square.shape, 1)
    square = jnp.where(sl < 32, square, 0.0) - jnp.where(sr == sl, 2.0, 0.0)
    gram = gram + dot(dot(proj_t[:, :32], square) + pick, known, nt=True)

    upper = gram
    inverse = onehot((ROWS, ROWS), lambda r, q: r == q)
    r8 = iota((ROWS, ROWS), 0)
    q8 = iota((ROWS, ROWS), 1)
    for p in range(block):
        pivot = upper[p:p + 1, p:p + 1]
        scale = lax.rsqrt(pivot)
        scale = scale * (1.5 - 0.5 * pivot * scale * scale)
        column = upper[:, p:p + 1] * scale
        row_u, row_i = upper[p:p + 1, :] * scale, inverse[p:p + 1, :] * scale
        upper = jnp.where(r8 == p, row_u, jnp.where(r8 > p, upper - column * row_u, upper))
        inverse = jnp.where(r8 == p, row_i, jnp.where(r8 > p, inverse - column * row_i, inverse))
    small_ref[0:ROWS, :] = proj_t
    small_ref[ROWS:2 * ROWS, 0:ROWS] = jnp.where(q8 >= r8, upper, 0.0)

    mix = dot(inverse, pick - proj_t)
    tall = dot(onehot((block * ROWS, ROWS), lambda r, q: (r >> 3) == q), mix)
    span = earlier * ROWS
    mix = split(diagonal(dot(tall, onehot((LANES, span), lambda r, q: (q >> 3) == r))))
    weights = [
        [
            jnp.broadcast_to(
                tall[k * ROWS:(k + 1) * ROWS, earlier + i:earlier + i + 1], (ROWS, LANES)
            )
            for i in range(k + 1)
        ]
        for k in range(block)
    ]
    for c in range(comp):
        out = dot_pieces(mix, [pieces[at, c] for at in range(3)])
        for x in range(width):
            for k in range(block):
                value = out[k * ROWS:(k + 1) * ROWS, LANES * x:LANES * (x + 1)]
                for i in range(k + 1):
                    value = value + weights[k][i] * allv[earlier + i, c, x]
                new_ref[k, c, x] = value

    @pl.loop(0, depth)
    def _(step):
        for kind in (0, 1):
            for side in (0, 1):
                @pl.when(has(kind, side, True))
                def _():
                    halo_copy(step, kind, side).wait_send()

    for at, stage in enumerate(stages):
        for offset in range(1, stage[2]):
            axis, digit, other, target = peer(stage, offset)
            pltpu.make_async_remote_copy(
                src_ref=mine.at[pl.ds(2 * at, 2)], dst_ref=gathered.at[at, digit],
                send_sem=red_send.at[at, other], recv_sem=red_recv.at[at, digit],
                device_id={axis: target}, device_id_type=MESH,
            ).wait_send()


def hand_over(rows, new_in, small, new_out, proj_out, tri_out):
    new_out[...] = new_in[...]
    proj_out[...] = small[: proj_out.shape[0], : proj_out.shape[1]]
    tri_out[...] = small[rows:rows + tri_out.shape[0], : tri_out.shape[1]]


def body(sizes, coefficients, earlier, start, shifts):
    coefficients = jnp.transpose(coefficients, (0, 1, 2, 4, 3, 5))
    earlier = jnp.transpose(earlier, (0, 1, 3, 2, 4))
    start = jnp.transpose(start, (0, 2, 1, 3))
    depth, count = shifts.shape[0], earlier.shape[0]
    block = depth + 1
    kinds, comp, _, width, rows, lanes = coefficients.shape
    stages = stages_of(sizes)
    most = max(stage[2] for stage in stages)
    f32 = jnp.float32
    anywhere = pl.BlockSpec(memory_space=pl.ANY)
    vmem = pl.BlockSpec(memory_space=pltpu.VMEM)
    new, small = pl.pallas_call(
        functools.partial(kernel, sizes),
        out_shape=(
            jax.ShapeDtypeStruct((block, comp, width, rows, lanes), f32),
            jax.ShapeDtypeStruct((2 * rows, lanes), f32),
        ),
        in_specs=[anywhere, anywhere, anywhere, pl.BlockSpec(memory_space=pltpu.SMEM)],
        out_specs=(vmem, vmem),
        scratch_shapes=[
            pltpu.VMEM(coefficients.shape, coefficients.dtype),
            pltpu.VMEM(coefficients.shape, f32),
            pltpu.VMEM((comp, comp, rows, lanes), f32),
            pltpu.VMEM((count + block, comp, width, rows, lanes), f32),
            pltpu.VMEM((3, comp, count * rows, width * lanes), jnp.bfloat16),
            pltpu.VMEM((comp, width, rows, lanes), f32),
            pltpu.VMEM((depth, 2, comp, rows, lanes), f32),
            pltpu.VMEM((depth, 2, 4 * comp, lanes), f32),
            pltpu.VMEM((depth, 2, 4 * comp, lanes), f32),
            pltpu.VMEM((count * rows, count * rows), f32),
            pltpu.VMEM((lanes, lanes), f32),
            pltpu.VMEM((2 * len(stages) + 2, rows, lanes), f32),
            pltpu.VMEM((len(stages), most, 2, rows, lanes), f32),
            pltpu.SemaphoreType.DMA((3,)),
            pltpu.SemaphoreType.DMA((depth, 2, 2)),
            pltpu.SemaphoreType.DMA((depth, 2, 2)),
            pltpu.SemaphoreType.DMA((len(stages), most)),
            pltpu.SemaphoreType.DMA((len(stages), most)),
        ],
        compiler_params=pltpu.CompilerParams(collective_id=0, has_side_effects=True),
        name="powers",
    )(coefficients, earlier, start, shifts)
    new, proj, tri = pl.pallas_call(
        functools.partial(hand_over, rows),
        out_shape=(
            jax.ShapeDtypeStruct(new.shape, f32),
            jax.ShapeDtypeStruct((block, count), f32),
            jax.ShapeDtypeStruct((block, block), f32),
        ),
        in_specs=[vmem, vmem],
        out_specs=(vmem, vmem, vmem),
        name="hand_over",
    )(new, small)
    return jnp.transpose(new, (0, 1, 3, 2, 4)), proj.T, tri


def solution(mesh):
    sizes = (("slab", mesh.shape["slab"]), ("sub", mesh.shape["sub"]))
    placed = (
        P(None, None, None, "slab", "sub", None),
        P(None, None, "slab", "sub", None),
        P(None, "slab", "sub", None),
        P(),
    )
    return jax.shard_map(
        functools.partial(body, sizes),
        mesh=mesh,
        in_specs=placed,
        out_specs=(P(None, None, "slab", "sub", None), P(), P()),
        check_vma=False,
    )
```
